256 devices in a mesh: blk: 64 (over z, y, x_hi), pb: 4 (over x_lo, core).
Axes of the slice: x: 4 (x_hi: 2, x_lo: 2; x = x_hi * 2 + x_lo), y: 4, z: 8, core: 2. Of those that a mesh axis runs over, the one named last changes fastest.
Arguments:
- query_rows: bfloat16 [81920, 1024], P(('blk', 'pb')), may hold values from -64 to 64
- key_rows: bfloat16 [81920, 1024], P(('blk', 'pb')), may hold values from -64 to 64
- partner: int32 [64, 1280], P('blk', 'pb'), may hold values from 0 to 1279, each once within a row
Outputs:
- pair_loss: float32 [81920], P(('blk', 'pb'))
- grad_queries: float32 [81920, 1024], P(('blk', 'pb'))
- grad_keys: float32 [81920, 1024], P(('blk', 'pb'))
The draws below stay inside these ranges and needn't reach their ends.
Inputs may be any that keep to these rules, and one draw needn't show every extreme that they name: Each row of partner is a permutation of 0 .. 1279.
All inputs are finite; a program needn't handle non-finite values.
Results may differ from the reference program's by a relative error of at most 0.0015.
Values may be sent and summed in bfloat16 or wider, within the bound.
A program may use at most 192 MiB of HBM per device.

```python
import math
import jax
import jax.numpy as jnp
from jax import lax

D = 1024
WIN = 4
BLK = 1280
BLOCKS = 64
ROWS = 81920


def draw_pair(key):
    base = jax.random.fold_in(key, 4099)
    streams = jax.random.split(base, 5)
    shape = (ROWS, D)
    query_base = jax.random.normal(streams[0], shape, jnp.float32)
    key_base = jax.random.normal(streams[1], shape, jnp.float32)
    query_scale = jnp.exp(jax.random.uniform(streams[3], (ROWS, 1), jnp.float32, math.log(0.3), math.log(3.0)))
    key_scale = jnp.exp(jax.random.uniform(streams[4], (ROWS, 1), jnp.float32, math.log(0.3), math.log(3.0)))
    query_out = query_base * query_scale
    key_out = key_base * key_scale
    return (query_out, key_out)


def draw_query_rows(key, part):
    return draw_pair(key)[0].astype(jnp.bfloat16)


def draw_key_rows(key, part):
    return draw_pair(key)[1].astype(jnp.bfloat16)


def setup_inputs(seed: int = 0) -> dict:
    keys = jax.random.split(jax.random.key(seed), 4)
    query_rows = draw_query_rows(jax.random.fold_in(keys[3], 71), 0)
    key_rows = draw_key_rows(jax.random.fold_in(keys[3], 71), 0)
    partner = jax.vmap(lambda own: jax.random.permutation(own, BLK))(jax.random.split(keys[2], BLOCKS)).reshape((BLOCKS, BLK)).astype(jnp.int32)
    return {"query_rows": query_rows, "key_rows": key_rows, "partner": partner}


def fetch(table, index):
    return lax.dynamic_index_in_dim(table, index, 0, keepdims=False)


def log_total(values, axes):
    top = jnp.max(values, axis=axes, keepdims=True)
    summed = jnp.sum(jnp.exp(values - top), axis=axes, keepdims=True)
    return jnp.squeeze(top + jnp.log(summed), axis=axes)


def reference(query_rows, key_rows, partner):
    factor = float(D) ** -0.5
    query_blocks = query_rows.reshape(BLOCKS, BLK, D)
    key_blocks = key_rows.reshape(BLOCKS, BLK, D)
    indices = jnp.arange(BLOCKS, dtype=jnp.int32)
    columns = jnp.arange(BLK, dtype=jnp.int32)

    def window_scores(index):
        query_block = fetch(query_blocks, index)
        blocks = [fetch(key_blocks, (index - step) % BLOCKS) for step in range(WIN)]
        scores = jnp.stack([jnp.dot(query_block, block.T, preferred_element_type=jnp.float32) * factor for block in blocks])
        return scores, blocks

    def first_pass(index):
        scores, blocks = window_scores(index)
        return log_total(scores, (0, 2)), log_total(scores, (1,))

    row_lse, col_part = lax.map(first_pass, indices)
    shifted = jnp.stack([jnp.roll(col_part[:, step], -step, axis=0) for step in range(WIN)])
    col_lse = log_total(shifted, (0,))

    def partner_mask(index):
        chosen = fetch(partner, index)
        return (columns[None, :] == chosen[:, None]).astype(jnp.float32), chosen

    def second_pass(index):
        scores, blocks = window_scores(index)
        own_lse = fetch(row_lse, index)
        col_window = jnp.stack([fetch(col_lse, (index - step) % BLOCKS) for step in range(WIN)])
        mask, chosen = partner_mask(index)
        weights = 0.5 * jnp.exp(scores - own_lse[None, :, None]) + 0.5 * jnp.exp(scores - col_window[:, None, :])
        weights = weights - jnp.stack([mask] + [jnp.zeros_like(mask)] * (WIN - 1))
        weights = weights.astype(jnp.bfloat16)
        summed = jnp.zeros((BLK, D), jnp.float32)
        for step in range(WIN):
            summed = summed + jnp.dot(weights[step], blocks[step], preferred_element_type=jnp.float32)
        positive = jnp.take_along_axis(scores[0], chosen[:, None], axis=1)[:, 0]
        loss = 0.5 * own_lse + 0.5 * jnp.take(col_window[0], chosen) - positive
        return loss, summed * factor

    def third_pass(index):
        key_block = fetch(key_blocks, index)
        key_lse = fetch(col_lse, index)
        summed = jnp.zeros((BLK, D), jnp.float32)
        for step in range(WIN):
            source = (index + step) % BLOCKS
            query_block = fetch(query_blocks, source)
            scores = jnp.dot(query_block, key_block.T, preferred_element_type=jnp.float32) * factor
            weights = 0.5 * jnp.exp(scores - fetch(row_lse, source)[:, None]) + 0.5 * jnp.exp(scores - key_lse[None, :])
            if step == 0:
                weights = weights - partner_mask(index)[0]
            weights = weights.astype(jnp.bfloat16)
            summed = summed + jnp.dot(weights.T, query_block, preferred_element_type=jnp.float32)
        return summed * factor

    pair_loss, grad_queries = lax.map(second_pass, indices)
    grad_keys = lax.map(third_pass, indices)
    return pair_loss.reshape(ROWS), grad_queries.reshape(ROWS, D), grad_keys.reshape(ROWS, D)
```

```python
import functools
import heapq

import jax
import jax.numpy as jnp
from jax import lax
from jax.experimental import pallas as pl
from jax.experimental.pallas import tpu as pltpu
from jax.sharding import PartitionSpec as P

WIN = 4
LANES = 128
LOG2E = 1.4426950408889634
LN2 = 0.6931471805599453
MESH = pl.DeviceIdType.MESH
TREES = "AAAB"
CHUNKS = len(TREES)
LINKS = {"P": 0, "M": 1, "V": 2, "C": 3}


def forwards(M, s, J, tree):
    out = []
    if tree == "A":
        if s == 0:
            if J == 0:
                out.append("P")
            out.append("V")
            if M == 0:
                out.append("M")
        elif s == 1:
            out.append("V")
        elif s == 2 and M == 1:
            out.append("M")
    else:
        if s == 0 and J == 0:
            out += ["P", "V"]
            if M == 0:
                out.append("M")
        elif s == 2 and J == 0:
            out.append("P")
            if M == 1:
                out.append("M")
        elif s == 1 and J == 1:
            out += ["P", "V"]
        elif s == 3 and J == 1:
            out.append("P")
    return out


def received(link, M, s, J):
    if link == "P":
        return (M, s, 1 - J)
    if link == "M":
        return (1 - M, 1, 1 - J)
    return (M, s + 2, J)


def depth(M, s, J, tree):
    return max([1 + depth(*received(k, M, s, J), tree) for k in forwards(M, s, J, tree)], default=0)


def plan(trees, total=14.5, lat=1.5, queue=2):
    chunks = len(trees)
    ct = total / chunks
    links = ["P", "M", "V0", "V1"]
    free = {k: 0.0 for k in links}
    flying = {k: [] for k in links}
    ready = {k: [] for k in links}
    ops, heap, count = [], [], [0]

    def have(M, s, J, n):
        for k in forwards(M, s, J, trees[n]):
            name = k if k != "V" else "V%d" % M
            count[0] += 1
            rank = -(1 + depth(*received(k, M, s, J), trees[n]))
            ready[name].append((rank, n, count[0], (k, M, s, J, n)))

    def fill(t):
        for k in links:
            flying[k] = [f for f in flying[k] if f > t + 1e-9]
            while ready[k] and len(flying[k]) < queue:
                ready[k].sort()
                item = ready[k].pop(0)[3]
                free[k] = max(free[k], t) + ct
                flying[k].append(free[k])
                ops.append(("send", t) + item)
                count[0] += 1
                heapq.heappush(heap, (free[k] + lat, count[0], received(*item[:4]) + (item[4],)))

    for n in range(chunks):
        for M in (1, 0):
            have(M, 0, 0, n)
    fill(0.0)
    while heap:
        t, _, item = heapq.heappop(heap)
        ops.append(("wait", t) + item)
        have(*item)
        fill(t)
    return ops


def with_tiles(ops, chunks, lag=2.5):
    out, left, due, done = [], {}, [], set()
    for M in (1, 0):
        left[(M, 0, 0)] = 0
        due.append((lag, (M, 0, 0)))
    for op in ops:
        ready = [d for d in due if d[0] <= op[1]]
        for d in ready:
            due.remove(d)
            out.append(("tile", op[1]) + d[1])
            done.add(d[1])
        out.append(op)
        if op[0] == "wait":
            key = op[2:5]
            left[key] = left.get(key, chunks) - 1
            if left[key] == 0:
                due.append((op[1] + lag, key))
    for d in sorted(due, key=lambda d: (-d[1][0], d[0])):
        out.append(("tile", d[0]) + d[1])
    return out


def kernel(
    blocks,
    q_hbm,
    k_hbm,
    partner_ref,
    loss_ref,
    gq_ref,
    gk_ref,
    win,
    sc,
    mx,
    sm,
    wb,
    colbuf,
    rowbuf,
    lse_col,
    par_col,
    lse_out,
    lse_in,
    par_out,
    par_in,
    load_sem,
    send_sem,
    ring_sem,
    core_sem,
    lse_send,
    lse_recv,
    par_send,
    par_recv,
):
    R, D = q_hbm.shape
    T = 2 * R
    CH = R // CHUNKS
    blk = lax.axis_index("blk")
    pb = lax.axis_index("pb")
    e = lax.rem(blk, 2)
    a = lax.div(pb, 2)
    core = lax.rem(pb, 2)
    mat = (e, 1 - e)
    cls = (a, 1 - a)
    own = pl.ds(pl.multiple_of(pb * R, 16), R)
    pair = (blk, pb + 2 - 4 * a)
    mate = (blk, pb + 1 - 2 * core)
    mirror = (blk + 1 - 2 * e, pb + 2 - 4 * a)
    cross = (blk, 3 - pb)
    up = (lax.rem(blk + 2, blocks), pb)
    down = (lax.rem(blk + blocks - 2, blocks), pb)

    load_q = pltpu.make_async_copy(q_hbm, win.at[1, 0, own], load_sem.at[0])
    load_k = pltpu.make_async_copy(k_hbm, win.at[0, 0, own], load_sem.at[1])
    load_q.start()
    load_k.start()
    barrier = pltpu.get_barrier_semaphore()
    for peer in (pair, mate, mirror, cross, up, down):
        pl.semaphore_signal(barrier, inc=1, device_id=peer, device_id_type=MESH)
    pl.semaphore_wait(barrier, 6)
    load_q.wait()
    load_k.wait()

    def slot(m, s, J, n, lane):
        at = pl.multiple_of((2 * cls[J] + lane) * R + n * CH, 16)
        return win.at[m, s, pl.ds(at, CH)]

    def copy(link, M, s, J, n):
        m, j = mat[M], cls[J]
        s_to = {"P": s, "M": 1, "V": s + 2, "C": s}[link]
        peer = {"P": pair, "M": mirror, "C": mate, "V": (lax.rem(blk + 2 - 4 * m + blocks, blocks), pb)}[link]
        sem = core_sem if link == "C" else ring_sem
        return pltpu.make_async_remote_copy(
            src_ref=slot(m, s, J, n, core),
            dst_ref=slot(m, s_to, J, n, core),
            send_sem=send_sem.at[LINKS[link], m, s, j, n],
            recv_sem=sem.at[m, s_to, j, n],
            device_id=peer,
            device_id_type=MESH,
        )

    def arrival(M, s, J, n, sem, lane, peer):
        m, j = mat[M], cls[J]
        ref = slot(m, s, J, n, lane)
        return pltpu.make_async_remote_copy(
            src_ref=ref,
            dst_ref=ref,
            send_sem=send_sem.at[0, m, s, j, n],
            recv_sem=sem.at[m, s, j, n],
            device_id=peer,
            device_id_type=MESH,
        )

    sent = []

    def start(link, M, s, J, n):
        c = copy(link, M, s, J, n)
        c.start()
        sent.append(c)

    def tile(M, s, J):
        m, j = mat[M], cls[J]
        for n in range(CHUNKS):
            arrival(M, s, J, n, core_sem, 1 - core, mate).wait_recv()
        rows = win[1 - m, 0, own, :]
        cols = win[m, s, pl.ds(pl.multiple_of(j * T, 16), T), :]
        x = lax.dot_general(rows, cols, (((1,), (1,)), ((), ())), preferred_element_type=jnp.float32)
        x = x * (LOG2E * float(D) ** -0.5)
        sc[m, s, j] = x
        parts = [x[:, g * LANES : (g + 1) * LANES] for g in range(T // LANES)]
        old = mx[m]
        new = functools.reduce(jnp.maximum, parts, old)
        total = sm[m] * jnp.exp2(old - new)
        for part in parts:
            total = total + jnp.exp2(part - new)
        mx[m] = new
        sm[m] = total

    def to_row(col):
        colbuf[pl.ds(pl.multiple_of(core * R, 8), R), :] = col
        return colbuf[...].T[0:1, :]

    ops = with_tiles(plan(TREES), CHUNKS)
    lead = [op for op in ops if op[0] == "send" and op[1] == 0.0]
    for op in lead:
        start(*op[2:])
    for n in range(CHUNKS):
        for M in (1, 0):
            start("C", M, 0, 0, n)

    colbuf[...] = jnp.zeros_like(colbuf)
    mx[...] = jnp.full_like(mx, -3.0e38)
    sm[...] = jnp.zeros_like(sm)
    rowbuf[...] = jnp.zeros_like(rowbuf)
    rowbuf[:, 0:R] = jnp.broadcast_to(partner_ref[...].astype(jnp.float32), (LANES, R))
    par_col[...] = rowbuf[...].T[0:R, :]
    row = to_row(par_col[...])
    par_out[...] = row
    par_in[pb] = row
    par_copies = []
    for i, peer in enumerate((pair, mate, cross)):
        c = pltpu.make_async_remote_copy(
            src_ref=par_out,
            dst_ref=par_in.at[pb],
            send_sem=par_send.at[i],
            recv_sem=par_recv.at[pb],
            device_id=peer,
            device_id_type=MESH,
        )
        c.start()
        par_copies.append(c)

    def lse_copy(m, s, t):
        peer = (lax.rem(blk + (2 * m - 1) * s + blocks, blocks), lax.rem(pb + t, 4))
        return pltpu.make_async_remote_copy(
            src_ref=lse_out.at[m],
            dst_ref=lse_in.at[1 - m, s, pb],
            send_sem=lse_send.at[m, s, t],
            recv_sem=lse_recv.at[1 - m, s, pb],
            device_id=peer,
            device_id_type=MESH,
        )

    lse_copies = []

    def finish(M):
        m = mat[M]
        high = mx[m]
        top = jnp.max(high, axis=1, keepdims=True)
        total = jnp.sum(sm[m] * jnp.exp2(high - top), axis=1, keepdims=True)
        lse = top + jnp.log(total) * LOG2E + 1.0
        full = jnp.broadcast_to(lse, (R, LANES))
        lse_col[m] = full
        out = to_row(full)
        lse_out[m] = out
        lse_in[1 - m, 0, pb] = out
        for s in range(WIN - 1, -1, -1):
            for t in range(4):
                if s or t:
                    c = lse_copy(m, s, t)
                    c.start()
                    lse_copies.append(c)

    waiting = {0: 4 * 2, 1: 4 * 2}
    for op in ops:
        if op[0] == "send":
            if op[1] > 0.0:
                start(*op[2:])
        elif op[0] == "wait":
            M, s, J, n = op[2:]
            arrival(M, s, J, n, ring_sem, core, pair).wait_recv()
            start("C", M, s, J, n)
        else:
            M = op[2]
            tile(*op[2:])
            waiting[M] -= 1
            if waiting[M] == 0:
                finish(M)

    for c in sent:
        c.wait_send()
    for c in par_copies:
        c.wait_send()
    for t in range(1, 4):
        p = lax.rem(pb + t, 4)
        pltpu.make_async_remote_copy(
            src_ref=par_out,
            dst_ref=par_in.at[p],
            send_sem=par_send.at[0],
            recv_sem=par_recv.at[p],
            device_id=pair,
            device_id_type=MESH,
        ).wait_recv()
    for m in range(2):
        for s in range(WIN):
            for t in range(4):
                if s or t:
                    p = lax.rem(pb + t, 4)
                    pltpu.make_async_remote_copy(
                        src_ref=lse_out.at[m],
                        dst_ref=lse_in.at[m, s, p],
                        send_sem=lse_send.at[m, s, t],
                        recv_sem=lse_recv.at[m, s, p],
                        device_id=pair,
                        device_id_type=MESH,
                    ).wait_recv()
    for c in lse_copies:
        c.wait_send()

    def weights(m, s):
        picked, partner_lse = [], []
        for j in range(2):
            c = lse_in[m, s, 2 * j] + lse_in[m, s, 2 * j + 1]
            if s == 0 and m == 1:
                chosen = par_in[2 * j] + par_in[2 * j + 1]
            for g in range(T // LANES):
                lanes = slice(g * LANES, (g + 1) * LANES)
                x = sc[m, s, j, :, lanes]
                cg = c[:, lanes]
                w = jnp.exp2(x - lse_col[m]) + jnp.exp2(x - cg)
                if s == 0:
                    if m == 0:
                        at = lax.broadcasted_iota(jnp.int32, (R, LANES), 1) + (j * T + g * LANES)
                        hit = at.astype(jnp.float32) == par_col[...]
                        picked.append(jnp.where(hit, x, 0.0))
                        partner_lse.append(jnp.where(hit, cg, 0.0))
                    else:
                        at = lax.broadcasted_iota(jnp.int32, (R, LANES), 0) + pb * R
                        hit = at.astype(jnp.float32) == chosen[:, lanes]
                    w = w - jnp.where(hit, 1.0, 0.0)
                wb[m, :, j * T + g * LANES : j * T + (g + 1) * LANES] = w.astype(jnp.bfloat16)
        if picked:
            score = jnp.sum(sum(picked), axis=1, keepdims=True)
            other = jnp.sum(sum(partner_lse), axis=1, keepdims=True)
            mine = lse_col[0][:, 0:1]
            loss = LN2 * (0.5 * (mine - 1.0) + 0.5 * (other - 1.0) - score)
            rowbuf2 = jnp.broadcast_to(loss, (R, LANES))
            colbuf[0:R, :] = rowbuf2
            loss_ref[...] = colbuf[...].T[0:1, 0:R]

    for s in range(WIN):
        for m, out in ((0, gq_ref), (1, gk_ref)):
            weights(m, s)
            part = jnp.dot(wb[m], win[m, s], preferred_element_type=jnp.float32) * float(D) ** -0.5
            if s == 0:
                out[...] = part
            else:
                out[...] += part


def local(blocks, query_rows, key_rows, partner):
    R, D = query_rows.shape
    T = 2 * R
    RP = (R + LANES - 1) // LANES * LANES
    f32, bf16 = jnp.float32, jnp.bfloat16
    dma = pltpu.SemaphoreType.DMA
    any_spec = pl.BlockSpec(memory_space=pl.ANY)
    vmem = pl.BlockSpec(memory_space=pltpu.VMEM)
    loss, grad_queries, grad_keys = pl.pallas_call(
        functools.partial(kernel, blocks),
        out_shape=(
            jax.ShapeDtypeStruct((1, R), f32),
            jax.ShapeDtypeStruct((R, D), f32),
            jax.ShapeDtypeStruct((R, D), f32),
        ),
        in_specs=[any_spec, any_spec, vmem],
        out_specs=[vmem, vmem, vmem],
        scratch_shapes=[
            pltpu.VMEM((2, WIN, 4 * R, D), bf16),
            pltpu.VMEM((2, WIN, 2, R, T), f32),
            pltpu.VMEM((2, R, LANES), f32),
            pltpu.VMEM((2, R, LANES), f32),
            pltpu.VMEM((2, R, 4 * R), bf16),
            pltpu.VMEM((T, LANES), f32),
            pltpu.VMEM((LANES, RP), f32),
            pltpu.VMEM((2, R, LANES), f32),
            pltpu.VMEM((R, LANES), f32),
            pltpu.VMEM((2, 1, T), f32),
            pltpu.VMEM((2, WIN, 4, 1, T), f32),
            pltpu.VMEM((1, T), f32),
            pltpu.VMEM((4, 1, T), f32),
            dma((2,)),
            dma((4, 2, WIN, 2, CHUNKS)),
            dma((2, WIN, 2, CHUNKS)),
            dma((2, WIN, 2, CHUNKS)),
            dma((2, WIN, 4)),
            dma((2, WIN, 4)),
            dma((3,)),
            dma((4,)),
        ],
        compiler_params=pltpu.CompilerParams(
            collective_id=0, has_side_effects=True, vmem_limit_bytes=58 * 1024 * 1024
        ),
        name="window_loss",
    )(query_rows, key_rows, partner)
    return loss.reshape(R), grad_queries, grad_keys


def solution(mesh):
    return jax.shard_map(
        functools.partial(local, mesh.shape["blk"]),
        mesh=mesh,
        in_specs=(P(("blk", "pb"), None), P(("blk", "pb"), None), P("blk", "pb")),
        out_specs=(P(("blk", "pb")), P(("blk", "pb"), None), P(("blk", "pb"), None)),
        check_vma=False,
    )
```

```python
import functools
import heapq

import jax
import jax.numpy as jnp
from jax import lax
from jax.experimental import pallas as pl
from jax.experimental.pallas import tpu as pltpu
from jax.sharding import PartitionSpec as P

WIN = 4
LANES = 128
LOG2E = 1.4426950408889634
LN2 = 0.6931471805599453
MESH = pl.DeviceIdType.MESH
TREES = "BAD"
SIZES = (48, 160, 112)
CHUNKS = len(TREES)
LINKS = {"P": 0, "M": 1, "V": 2, "C": 3}
PRIORITY = {
    "P": ((3.2, 3.7, 0.4, 1.3), (3.6, 0.3, 1.4, 4.2)),
    "M": ((2.3, 0.0, 0.0, 0.0), (0.0, 0.0, 2.2, 0.0)),
    "V0": ((2.0, 0.7, 0.0, 0.0), (0.0, 0.0, 0.0, 0.0)),
    "V1": ((0.0, 0.0, 0.0, 0.0), (2.6, 3.1, 0.0, 0.0)),
}
LATENCY = {"P": 1.7, "M": 2.0, "V": 2.6}


def forwards(M, s, J, tree):
    out = []
    if s == 0:
        if J == 0:
            out.append("P")
        if J == 0 or tree != "B":
            out.append("V")
            if M == 0:
                out.append("M")
    elif s == 1:
        if tree == "A":
            out.append("V")
        elif J == 1:
            out += ["P", "V"] if tree == "B" else ["V"]
    elif s == 2:
        if tree == "B" and J == 0:
            out.append("P")
        if M == 1 and (J == 0 or tree != "B"):
            out.append("M")
    elif J == 1 and tree != "A":
        out.append("P")
    return out


def received(link, M, s, J):
    if link == "P":
        return (M, s, 1 - J)
    if link == "M":
        return (1 - M, 1, 1 - J)
    return (M, s + 2, J)


def plan(trees, queue=2):
    chunks = len(trees)
    ct = [2 * (rows * 2048e-5 + 0.15) for rows in SIZES]
    links = ["P", "M", "V0", "V1"]
    free = {k: 0.0 for k in links}
    flying = {k: [] for k in links}
    ready = {k: [] for k in links}
    ops, heap, count = [], [], [0]

    def have(M, s, J, n):
        for k in forwards(M, s, J, trees[n]):
            name = k if k != "V" else "V%d" % M
            ready[name].append((n - PRIORITY[name][M][s], n, J, (k, M, s, J, n)))

    def fill(t):
        for k in links:
            flying[k] = [f for f in flying[k] if f > t + 1e-9]
            while ready[k] and len(flying[k]) < queue:
                ready[k].sort()
                item = ready[k].pop(0)[3]
                free[k] = max(free[k], t) + ct[item[4]]
                flying[k].append(free[k])
                ops.append(("send", t) + item)
                count[0] += 1
                heapq.heappush(heap, (free[k] + LATENCY[item[0]], count[0], received(*item[:4]) + (item[4],)))

    for n in range(chunks):
        for M in (1, 0):
            have(M, 0, 0, n)
    fill(0.0)
    while heap:
        t, _, item = heapq.heappop(heap)
        ops.append(("wait", t) + item)
        have(*item)
        fill(t)
    return ops


def with_tiles(ops, chunks, lag=1.6):
    out, left, due, done = [], {}, [], set()
    for M in (1, 0):
        left[(M, 0, 0)] = 0
        due.append((lag, (M, 0, 0)))
    for op in ops:
        ready = [d for d in due if d[0] <= op[1]]
        for d in ready:
            due.remove(d)
            out.append(("tile", op[1]) + d[1])
            done.add(d[1])
        out.append(op)
        if op[0] == "wait":
            key = op[2:5]
            left[key] = left.get(key, chunks) - 1
            if left[key] == 0:
                due.append((op[1] + lag, key))
    for d in sorted(due, key=lambda d: (-d[1][0], d[0])):
        out.append(("tile", d[0]) + d[1])
    return out


def kernel(
    blocks,
    q_hbm,
    k_hbm,
    partner_hbm,
    loss_ref,
    grad_ref,
    win,
    sc,
    mx,
    sm,
    wb,
    colbuf,
    rowbuf,
    lse_col,
    par_col,
    lse_out,
    lse_in,
    par_out,
    par_in,
    partner_ref,
    load_sem,
    send_sem,
    ring_sem,
    core_sem,
    lse_send,
    lse_recv,
    par_send,
    par_recv,
):
    R, D = q_hbm.shape
    T = 2 * R
    starts = [sum(SIZES[:n]) for n in range(CHUNKS)]
    assert sum(SIZES) == R
    blk = lax.axis_index("blk")
    pb = lax.axis_index("pb")
    e = lax.rem(blk, 2)
    a = lax.div(pb, 2)
    core = lax.rem(pb, 2)
    mat = (e, 1 - e)
    cls = (a, 1 - a)
    own = pl.ds(pl.multiple_of(pb * R, 16), R)
    pair = (blk, pb + 2 - 4 * a)
    mate = (blk, pb + 1 - 2 * core)
    mirror = (blk + 1 - 2 * e, pb + 2 - 4 * a)
    cross = (blk, 3 - pb)
    up = (lax.rem(blk + 2, blocks), pb)
    down = (lax.rem(blk + blocks - 2, blocks), pb)

    load_q = pltpu.make_async_copy(q_hbm, win.at[1, 0, own], load_sem.at[0])
    load_k = pltpu.make_async_copy(k_hbm, win.at[0, 0, own], load_sem.at[1])
    load_p = pltpu.make_async_copy(partner_hbm, partner_ref, load_sem.at[2])
    load_q.start()
    load_k.start()
    load_p.start()
    barrier = pltpu.get_barrier_semaphore()
    for peer in (pair, mate, mirror, cross, up, down):
        pl.semaphore_signal(barrier, inc=1, device_id=peer, device_id_type=MESH)
    pl.semaphore_wait(barrier, 6)
    load_q.wait()
    load_k.wait()
    load_p.wait()

    def slot(m, s, J, n, lane):
        at = pl.multiple_of((2 * cls[J] + lane) * R + starts[n], 16)
        return win.at[m, s, pl.ds(at, SIZES[n])]

    def copy(link, M, s, J, n):
        m, j = mat[M], cls[J]
        s_to = {"P": s, "M": 1, "V": s + 2, "C": s}[link]
        peer = {"P": pair, "M": mirror, "C": mate, "V": (lax.rem(blk + 2 - 4 * m + blocks, blocks), pb)}[link]
        sem = core_sem if link == "C" else ring_sem
        return pltpu.make_async_remote_copy(
            src_ref=slot(m, s, J, n, core),
            dst_ref=slot(m, s_to, J, n, core),
            send_sem=send_sem.at[LINKS[link], m, s, j, n],
            recv_sem=sem.at[m, s_to, j, n],
            device_id=peer,
            device_id_type=MESH,
        )

    def arrival(M, s, J, n, sem, lane, peer):
        m, j = mat[M], cls[J]
        ref = slot(m, s, J, n, lane)
        return pltpu.make_async_remote_copy(
            src_ref=ref,
            dst_ref=ref,
            send_sem=send_sem.at[0, m, s, j, n],
            recv_sem=sem.at[m, s, j, n],
            device_id=peer,
            device_id_type=MESH,
        )

    sent = []

    def start(link, M, s, J, n):
        c = copy(link, M, s, J, n)
        c.start()
        sent.append(c)

    def tile(M, s, J):
        m, j = mat[M], cls[J]
        for n in range(CHUNKS):
            arrival(M, s, J, n, core_sem, 1 - core, mate).wait_recv()
        rows = win[1 - m, 0, own, :]
        cols = win[m, s, pl.ds(pl.multiple_of(j * T, 16), T), :]
        x = lax.dot_general(rows, cols, (((1,), (1,)), ((), ())), preferred_element_type=jnp.float32)
        x = x * (LOG2E * float(D) ** -0.5)
        sc[m, s, j] = x
        parts = [x[:, g * LANES : (g + 1) * LANES] for g in range(T // LANES)]
        old = mx[m]
        new = functools.reduce(jnp.maximum, parts, old)
        total = sm[m] * jnp.exp2(old - new)
        for part in parts:
            total = total + jnp.exp2(part - new)
        mx[m] = new
        sm[m] = total

    def to_row(col):
        colbuf[pl.ds(pl.multiple_of(core * R, 8), R), :] = col
        return colbuf[...].T[0:1, :]

    ops = with_tiles(plan(TREES), CHUNKS)
    lead = [op for op in ops if op[0] == "send" and op[1] == 0.0]
    for op in lead:
        start(*op[2:])
    for n in range(CHUNKS):
        for M in (1, 0):
            start("C", M, 0, 0, n)

    colbuf[...] = jnp.zeros_like(colbuf)
    mx[...] = jnp.full_like(mx, -3.0e38)
    sm[...] = jnp.zeros_like(sm)
    rowbuf[...] = jnp.zeros_like(rowbuf)
    rowbuf[:, 0:R] = jnp.broadcast_to(partner_ref[...].astype(jnp.float32), (LANES, R))
    par_col[...] = rowbuf[...].T[0:R, :]
    row = to_row(par_col[...])
    par_out[...] = row
    par_in[pb] = row
    par_copies = []
    for i, peer in enumerate((pair, mate, cross)):
        c = pltpu.make_async_remote_copy(
            src_ref=par_out,
            dst_ref=par_in.at[pb],
            send_sem=par_send.at[i],
            recv_sem=par_recv.at[pb],
            device_id=peer,
            device_id_type=MESH,
        )
        c.start()
        par_copies.append(c)

    def lse_copy(m, s, t):
        peer = (lax.rem(blk + (2 * m - 1) * s + blocks, blocks), lax.rem(pb + t, 4))
        return pltpu.make_async_remote_copy(
            src_ref=lse_out.at[m],
            dst_ref=lse_in.at[1 - m, s, pb],
            send_sem=lse_send.at[m, s, t],
            recv_sem=lse_recv.at[1 - m, s, pb],
            device_id=peer,
            device_id_type=MESH,
        )

    lse_copies = []

    def finish(M):
        m = mat[M]
        high = mx[m]
        top = jnp.max(high, axis=1, keepdims=True)
        total = jnp.sum(sm[m] * jnp.exp2(high - top), axis=1, keepdims=True)
        lse = top + jnp.log(total) * LOG2E + 1.0
        full = jnp.broadcast_to(lse, (R, LANES))
        lse_col[m] = full
        out = to_row(full)
        lse_out[m] = out
        lse_in[1 - m, 0, pb] = out
        for s in range(WIN - 1, -1, -1):
            for t in range(4):
                if s or t:
                    c = lse_copy(m, s, t)
                    c.start()
                    lse_copies.append(c)

    waiting = {0: 4 * 2, 1: 4 * 2}
    for op in ops:
        if op[0] == "send":
            if op[1] > 0.0:
                start(*op[2:])
        elif op[0] == "wait":
            M, s, J, n = op[2:]
            arrival(M, s, J, n, ring_sem, core, pair).wait_recv()
            start("C", M, s, J, n)
        else:
            M = op[2]
            tile(*op[2:])
            waiting[M] -= 1
            if waiting[M] == 0:
                finish(M)

    for c in sent:
        c.wait_send()
    for c in par_copies:
        c.wait_send()
    for t in range(1, 4):
        p = lax.rem(pb + t, 4)
        pltpu.make_async_remote_copy(
            src_ref=par_out,
            dst_ref=par_in.at[p],
            send_sem=par_send.at[0],
            recv_sem=par_recv.at[p],
            device_id=pair,
            device_id_type=MESH,
        ).wait_recv()
    def lse_wait(M, s):
        m = mat[M]
        for t in range(4):
            if s or t:
                p = lax.rem(pb + t, 4)
                pltpu.make_async_remote_copy(
                    src_ref=lse_out.at[m],
                    dst_ref=lse_in.at[m, s, p],
                    send_sem=lse_send.at[m, s, t],
                    recv_sem=lse_recv.at[m, s, p],
                    device_id=pair,
                    device_id_type=MESH,
                ).wait_recv()

    def gradient(M, s, first):
        m = mat[M]
        keys = mat[M] == 0
        for j in range(2):
            c = lse_in[m, s, 2 * j] + lse_in[m, s, 2 * j + 1]
            if s == 0:
                chosen = par_in[2 * j] + par_in[2 * j + 1]
            for g in range(T // LANES):
                lanes = slice(g * LANES, (g + 1) * LANES)
                x = sc[m, s, j, :, lanes]
                w = jnp.exp2(x - lse_col[m]) + jnp.exp2(x - c[:, lanes])
                if s == 0:
                    col = lax.broadcasted_iota(jnp.int32, (R, LANES), 1) + (j * T + g * LANES)
                    row = lax.broadcasted_iota(jnp.int32, (R, LANES), 0) + pb * R
                    at = jnp.where(keys, col, row).astype(jnp.float32)
                    hit = at == jnp.where(keys, par_col[...], jnp.broadcast_to(chosen[:, lanes], (R, LANES)))
                    w = w - jnp.where(hit, 1.0, 0.0)
                wb[m, :, j * T + g * LANES : j * T + (g + 1) * LANES] = w.astype(jnp.bfloat16)
        part = jnp.dot(wb[m], win[m, s], preferred_element_type=jnp.float32)
        if first:
            grad_ref[m] = part
        else:
            grad_ref[m] += part

    for M, s in ((1, 1), (1, 3), (0, 0), (0, 2)):
        lse_wait(M, s)
    gradient(1, 1, True)
    gradient(0, 0, True)
    gradient(1, 3, False)
    gradient(0, 2, False)
    for M, s in ((1, 0), (1, 2), (0, 1), (0, 3)):
        lse_wait(M, s)
    for c in lse_copies:
        c.wait_send()
    gradient(1, 2, False)
    gradient(0, 1, False)
    gradient(1, 0, False)
    gradient(0, 3, False)

    picked = jnp.zeros((R, LANES), jnp.float32)
    partner_lse = picked
    for j in range(2):
        c = lse_in[0, 0, 2 * j] + lse_in[0, 0, 2 * j + 1]
        for g in range(T // LANES):
            lanes = slice(g * LANES, (g + 1) * LANES)
            col = lax.broadcasted_iota(jnp.int32, (R, LANES), 1) + (j * T + g * LANES)
            hit = col.astype(jnp.float32) == par_col[...]
            picked += jnp.where(hit, sc[0, 0, j, :, lanes], 0.0)
            partner_lse += jnp.where(hit, jnp.broadcast_to(c[:, lanes], (R, LANES)), 0.0)
    score = jnp.sum(picked, axis=1, keepdims=True)
    other = jnp.sum(partner_lse, axis=1, keepdims=True)
    mine = lse_col[0][:, 0:1]
    loss = LN2 * (0.5 * (mine - 1.0) + 0.5 * (other - 1.0) - score)
    colbuf[0:R, :] = jnp.broadcast_to(loss, (R, LANES))
    loss_ref[...] = colbuf[...].T[0:1, 0:R]


def local(blocks, query_rows, key_rows, partner):
    query_rows = pltpu.with_memory_space_constraint(query_rows, pltpu.HBM)
    key_rows = pltpu.with_memory_space_constraint(key_rows, pltpu.HBM)
    partner = pltpu.with_memory_space_constraint(partner, pltpu.HBM)
    R, D = query_rows.shape
    T = 2 * R
    RP = (R + LANES - 1) // LANES * LANES
    f32, bf16 = jnp.float32, jnp.bfloat16
    dma = pltpu.SemaphoreType.DMA
    hbm = pl.BlockSpec(memory_space=pltpu.HBM)
    vmem = pl.BlockSpec(memory_space=pltpu.VMEM)
    loss, grads = pl.pallas_call(
        functools.partial(kernel, blocks),
        out_shape=(
            jax.ShapeDtypeStruct((1, R), f32),
            jax.ShapeDtypeStruct((2, R, D), f32),
        ),
        in_specs=[hbm, hbm, hbm],
        out_specs=[vmem, vmem],
        scratch_shapes=[
            pltpu.VMEM((2, WIN, 4 * R, D), bf16),
            pltpu.VMEM((2, WIN, 2, R, T), f32),
            pltpu.VMEM((2, R, LANES), f32),
            pltpu.VMEM((2, R, LANES), f32),
            pltpu.VMEM((2, R, 4 * R), bf16),
            pltpu.VMEM((T, LANES), f32),
            pltpu.VMEM((LANES, RP), f32),
            pltpu.VMEM((2, R, LANES), f32),
            pltpu.VMEM((R, LANES), f32),
            pltpu.VMEM((2, 1, T), f32),
            pltpu.VMEM((2, WIN, 4, 1, T), f32),
            pltpu.VMEM((1, T), f32),
            pltpu.VMEM((4, 1, T), f32),
            pltpu.VMEM((1, R), jnp.int32),
            dma((3,)),
            dma((4, 2, WIN, 2, CHUNKS)),
            dma((2, WIN, 2, CHUNKS)),
            dma((2, WIN, 2, CHUNKS)),
            dma((2, WIN, 4)),
            dma((2, WIN, 4)),
            dma((3,)),
            dma((4,)),
        ],
        compiler_params=pltpu.CompilerParams(
            collective_id=0, has_side_effects=True, vmem_limit_bytes=46 * 1024 * 1024
        ),
        name="window_loss",
    )(query_rows, key_rows, partner)
    factor = float(D) ** -0.5
    return loss.reshape(R), grads[0] * factor, grads[1] * factor


def solution(mesh):
    return jax.shard_map(
        functools.partial(local, mesh.shape["blk"]),
        mesh=mesh,
        in_specs=(P(("blk", "pb"), None), P(("blk", "pb"), None), P("blk", "pb")),
        out_specs=(P(("blk", "pb")), P(("blk", "pb"), None), P(("blk", "pb"), None)),
        check_vma=False,
    )
```

```python
import functools
import heapq

import jax
import jax.numpy as jnp
from jax import lax
from jax.experimental import pallas as pl
from jax.experimental.pallas import tpu as pltpu
from jax.sharding import PartitionSpec as P

WIN = 4
LANES = 128
LOG2E = 1.4426950408889634
LN2 = 0.6931471805599453
MESH = pl.DeviceIdType.MESH
TREES = "ADC"
SIZES = (48, 176, 96)
CHUNKS = len(TREES)
LINKS = {"P": 0, "M": 1, "V": 2, "C": 3}
PRIORITY = {
    "P": ((0.6, 3.4, 4.1, 3.0), (0.2, 1.1, 3.9, 2.4)),
    "M": ((1.3, 0.0, 0.0, 0.0), (0.0, 0.0, 4.9, 0.0)),
    "V0": ((0.9, 1.7, 0.0, 0.0), (0.0, 0.0, 0.0, 0.0)),
    "V1": ((0.0, 0.0, 0.0, 0.0), (0.3, 1.6, 0.0, 0.0)),
}
LAGS = (4.0, 4.0)
LATENCY = {"P": 1.7, "M": 2.0, "V": 2.6}


def forwards(M, s, J, tree):
    own = M == 0
    if s == 0:
        if J == 0:
            return ["P", "V", "M"] if own else ["P", "V"]
        if tree == "B":
            return []
        return ["V", "M"] if own and tree != "C" else ["V"]
    if s == 1:
        if tree == "A" or tree == "D":
            return ["V"] if J == 1 or tree == "A" else []
        if J == 1:
            return ["P", "V"]
        return ["V"] if tree == "C" else []
    if s == 2:
        out = ["P"] if tree == "B" and J == 0 else []
        if not own and (J == 0 or tree in "AD"):
            out.append("M")
        return out
    return ["P"] if J == 1 and tree in "BD" else []


def received(link, M, s, J):
    if link == "P":
        return (M, s, 1 - J)
    if link == "M":
        return (1 - M, 1, 1 - J)
    return (M, s + 2, J)


def plan(trees, queue=2):
    chunks = len(trees)
    ct = [2 * (rows * 2048e-5 + 0.15) for rows in SIZES]
    links = ["P", "M", "V0", "V1"]
    free = {k: 0.0 for k in links}
    flying = {k: [] for k in links}
    ready = {k: [] for k in links}
    ops, heap, count = [], [], [0]

    def have(M, s, J, n):
        for k in forwards(M, s, J, trees[n]):
            name = k if k != "V" else "V%d" % M
            ready[name].append((n - PRIORITY[name][M][s], n, J, (k, M, s, J, n)))

    def fill(t):
        for k in links:
            flying[k] = [f for f in flying[k] if f > t + 1e-9]
            while ready[k] and len(flying[k]) < queue:
                ready[k].sort()
                item = ready[k].pop(0)[3]
                free[k] = max(free[k], t) + ct[item[4]]
                flying[k].append(free[k])
                ops.append(("send", t) + item)
                count[0] += 1
                heapq.heappush(heap, (free[k] + LATENCY[item[0]], count[0], received(*item[:4]) + (item[4],)))

    for n in range(chunks):
        for M in (1, 0):
            have(M, 0, 0, n)
    fill(0.0)
    while heap:
        t, _, item = heapq.heappop(heap)
        ops.append(("wait", t) + item)
        have(*item)
        fill(t)
    return ops


def with_tiles(ops, chunks, lags):
    out, left, due = [], {}, []
    for M in (1, 0):
        left[(M, 0, 0)] = 0
        due.append((lags[M], (M, 0, 0)))
    for op in ops:
        ready = [d for d in due if d[0] <= op[1]]
        for d in ready:
            due.remove(d)
            out.append(("tile", op[1]) + d[1])
        out.append(op)
        if op[0] == "wait":
            key = op[2:5]
            left[key] = left.get(key, chunks) - 1
            if left[key] == 0:
                due.append((op[1] + lags[op[2]], key))
    for d in sorted(due, key=lambda d: (-d[1][0], d[0])):
        out.append(("tile", d[0]) + d[1])
    return out


def kernel(
    blocks,
    q_hbm,
    k_hbm,
    partner_hbm,
    loss_ref,
    grad_ref,
    win,
    sc,
    mx,
    sm,
    wb,
    colbuf,
    rowbuf,
    lse_col,
    par_col,
    lse_out,
    lse_in,
    par_out,
    par_in,
    partner_ref,
    load_sem,
    send_sem,
    ring_sem,
    core_sem,
    lse_send,
    lse_recv,
    par_send,
    par_recv,
):
    R, D = q_hbm.shape
    T = 2 * R
    starts = [sum(SIZES[:n]) for n in range(CHUNKS)]
    assert sum(SIZES) == R
    blk = lax.axis_index("blk")
    pb = lax.axis_index("pb")
    e = lax.rem(blk, 2)
    a = lax.div(pb, 2)
    core = lax.rem(pb, 2)
    mat = (e, 1 - e)
    cls = (a, 1 - a)
    own = pl.ds(pl.multiple_of(pb * R, 16), R)
    pair = (blk, pb + 2 - 4 * a)
    mate = (blk, pb + 1 - 2 * core)
    mirror = (blk + 1 - 2 * e, pb + 2 - 4 * a)
    cross = (blk, 3 - pb)
    up = (lax.rem(blk + 2, blocks), pb)
    down = (lax.rem(blk + blocks - 2, blocks), pb)

    load_q = pltpu.make_async_copy(q_hbm, win.at[1, 0, own], load_sem.at[0])
    load_k = pltpu.make_async_copy(k_hbm, win.at[0, 0, own], load_sem.at[1])
    load_p = pltpu.make_async_copy(partner_hbm, partner_ref, load_sem.at[2])
    load_q.start()
    load_k.start()
    load_p.start()
    barrier = pltpu.get_barrier_semaphore()
    for peer in (pair, mate, mirror, cross, up, down):
        pl.semaphore_signal(barrier, inc=1, device_id=peer, device_id_type=MESH)
    pl.semaphore_wait(barrier, 6)
    load_q.wait()
    load_k.wait()
    load_p.wait()

    def slot(m, s, J, n, lane):
        at = pl.multiple_of((2 * cls[J] + lane) * R + starts[n], 16)
        return win.at[m, s, pl.ds(at, SIZES[n])]

    def copy(link, M, s, J, n):
        m, j = mat[M], cls[J]
        s_to = {"P": s, "M": 1, "V": s + 2, "C": s}[link]
        peer = {"P": pair, "M": mirror, "C": mate, "V": (lax.rem(blk + 2 - 4 * m + blocks, blocks), pb)}[link]
        sem = core_sem if link == "C" else ring_sem
        return pltpu.make_async_remote_copy(
            src_ref=slot(m, s, J, n, core),
            dst_ref=slot(m, s_to, J, n, core),
            send_sem=send_sem.at[LINKS[link], m, s, j, n],
            recv_sem=sem.at[m, s_to, j, n],
            device_id=peer,
            device_id_type=MESH,
        )

    def arrival(M, s, J, n, sem, lane, peer):
        m, j = mat[M], cls[J]
        ref = slot(m, s, J, n, lane)
        return pltpu.make_async_remote_copy(
            src_ref=ref,
            dst_ref=ref,
            send_sem=send_sem.at[0, m, s, j, n],
            recv_sem=sem.at[m, s, j, n],
            device_id=peer,
            device_id_type=MESH,
        )

    sent = []

    def start(t, link, M, s, J, n):
        c = copy(link, M, s, J, n)
        c.start()
        sent.append((t, c))

    def settle(t):
        while sent and sent[0][0] + 14.0 < t:
            sent.pop(0)[1].wait_send()

    def tile(M, s, J):
        m, j = mat[M], cls[J]
        for n in range(CHUNKS):
            arrival(M, s, J, n, core_sem, 1 - core, mate).wait_recv()
        rows = win[1 - m, 0, own, :]
        cols = win[m, s, pl.ds(pl.multiple_of(j * T, 16), T), :]
        x = lax.dot_general(rows, cols, (((1,), (1,)), ((), ())), preferred_element_type=jnp.float32)
        x = x * (LOG2E * float(D) ** -0.5)
        sc[m, s, j] = x
        parts = [x[:, g * LANES : (g + 1) * LANES] for g in range(T // LANES)]
        old = mx[m]
        new = functools.reduce(jnp.maximum, parts, old)
        total = sm[m] * jnp.exp2(old - new)
        for part in parts:
            total = total + jnp.exp2(part - new)
        mx[m] = new
        sm[m] = total

    def to_row(col):
        colbuf[pl.ds(pl.multiple_of(core * R, 8), R), :] = col
        return colbuf[...].T[0:1, :]

    ops = with_tiles(plan(TREES), CHUNKS, LAGS)
    lead = [op for op in ops if op[0] == "send" and op[1] == 0.0]
    for op in lead:
        start(*op[1:])
    for n in range(CHUNKS):
        for M in (1, 0):
            start(0.0, "C", M, 0, 0, n)

    colbuf[...] = jnp.zeros_like(colbuf)
    mx[...] = jnp.full_like(mx, -3.0e38)
    sm[...] = jnp.zeros_like(sm)
    rowbuf[...] = jnp.zeros_like(rowbuf)
    rowbuf[:, 0:R] = jnp.broadcast_to(partner_ref[...].astype(jnp.float32), (LANES, R))
    par_col[...] = rowbuf[...].T[0:R, :]
    row = to_row(par_col[...])
    par_out[...] = row
    par_in[pb] = row
    par_copies = []
    for i, peer in enumerate((pair, mate, cross)):
        c = pltpu.make_async_remote_copy(
            src_ref=par_out,
            dst_ref=par_in.at[pb],
            send_sem=par_send.at[i],
            recv_sem=par_recv.at[pb],
            device_id=peer,
            device_id_type=MESH,
        )
        c.start()
        par_copies.append(c)

    def lse_copy(m, s, t):
        peer = (lax.rem(blk + (2 * m - 1) * s + blocks, blocks), lax.rem(pb + t, 4))
        return pltpu.make_async_remote_copy(
            src_ref=lse_out.at[m],
            dst_ref=lse_in.at[1 - m, s, pb],
            send_sem=lse_send.at[m, s, t],
            recv_sem=lse_recv.at[1 - m, s, pb],
            device_id=peer,
            device_id_type=MESH,
        )

    lse_copies = []

    def finish(M):
        m = mat[M]
        high = mx[m]
        top = jnp.max(high, axis=1, keepdims=True)
        total = jnp.sum(sm[m] * jnp.exp2(high - top), axis=1, keepdims=True)
        lse = top + jnp.log(total) * LOG2E + 1.0
        full = jnp.broadcast_to(lse, (R, LANES))
        lse_col[m] = full
        out = to_row(full)
        lse_out[m] = out
        lse_in[1 - m, 0, pb] = out
        for s in range(WIN - 1, -1, -1):
            for t in range(4):
                if s or t:
                    c = lse_copy(m, s, t)
                    c.start()
                    lse_copies.append(c)

    waiting = {0: 4 * 2, 1: 4 * 2}
    for op in ops:
        if op[0] == "send":
            if op[1] > 0.0:
                start(*op[1:])
        elif op[0] == "wait":
            M, s, J, n = op[2:]
            arrival(M, s, J, n, ring_sem, core, pair).wait_recv()
            start(op[1], "C", M, s, J, n)
            settle(op[1])
        else:
            M = op[2]
            tile(*op[2:])
            waiting[M] -= 1
            if waiting[M] == 0:
                finish(M)

    for t in range(1, 4):
        p = lax.rem(pb + t, 4)
        pltpu.make_async_remote_copy(
            src_ref=par_out,
            dst_ref=par_in.at[p],
            send_sem=par_send.at[0],
            recv_sem=par_recv.at[p],
            device_id=pair,
            device_id_type=MESH,
        ).wait_recv()
    def lse_wait(M, s):
        m = mat[M]
        for t in range(4):
            if s or t:
                p = lax.rem(pb + t, 4)
                pltpu.make_async_remote_copy(
                    src_ref=lse_out.at[m],
                    dst_ref=lse_in.at[m, s, p],
                    send_sem=lse_send.at[m, s, t],
                    recv_sem=lse_recv.at[m, s, p],
                    device_id=pair,
                    device_id_type=MESH,
                ).wait_recv()

    def weights(k, M, s):
        m = mat[M]
        keys = mat[M] == 0
        for j in range(2):
            c = lse_in[m, s, 2 * j] + lse_in[m, s, 2 * j + 1]
            if s == 0:
                chosen = par_in[2 * j] + par_in[2 * j + 1]
            for g in range(T // LANES):
                lanes = slice(g * LANES, (g + 1) * LANES)
                x = sc[m, s, j, :, lanes]
                w = jnp.exp2(x - lse_col[m]) + jnp.exp2(x - c[:, lanes])
                if s == 0:
                    col = lax.broadcasted_iota(jnp.int32, (R, LANES), 1) + (j * T + g * LANES)
                    row = lax.broadcasted_iota(jnp.int32, (R, LANES), 0) + pb * R
                    at = jnp.where(keys, col, row).astype(jnp.float32)
                    hit = at == jnp.where(keys, par_col[...], jnp.broadcast_to(chosen[:, lanes], (R, LANES)))
                    w = w - jnp.where(hit, 1.0, 0.0)
                wb[k % 2, :, j * T + g * LANES : j * T + (g + 1) * LANES] = w.astype(jnp.bfloat16)

    def product(k, M, s, first):
        m = mat[M]
        part = jnp.dot(wb[k % 2], win[m, s], preferred_element_type=jnp.float32)
        if first:
            grad_ref[m] = part
        else:
            grad_ref[m] += part

    def losses():
        picked = jnp.zeros((R, LANES), jnp.float32)
        partner_lse = picked
        for j in range(2):
            c = lse_in[0, 0, 2 * j] + lse_in[0, 0, 2 * j + 1]
            for g in range(T // LANES):
                lanes = slice(g * LANES, (g + 1) * LANES)
                col = lax.broadcasted_iota(jnp.int32, (R, LANES), 1) + (j * T + g * LANES)
                hit = col.astype(jnp.float32) == par_col[...]
                picked += jnp.where(hit, sc[0, 0, j, :, lanes], 0.0)
                partner_lse += jnp.where(hit, jnp.broadcast_to(c[:, lanes], (R, LANES)), 0.0)
        score = jnp.sum(picked, axis=1, keepdims=True)
        other = jnp.sum(partner_lse, axis=1, keepdims=True)
        mine = lse_col[0][:, 0:1]
        loss = LN2 * (0.5 * (mine - 1.0) + 0.5 * (other - 1.0) - score)
        colbuf[0:R, :] = jnp.broadcast_to(loss, (R, LANES))
        loss_ref[...] = colbuf[...].T[0:1, 0:R]

    order = ((0, 0), (0, 2), (1, 1), (1, 3), (1, 0), (1, 2), (0, 1), (0, 3))
    lse_wait(*order[0])
    weights(0, *order[0])
    seen = set()
    for k, (M, s) in enumerate(order):
        if k + 1 < len(order):
            lse_wait(*order[k + 1])
        product(k, M, s, M not in seen)
        seen.add(M)
        if k + 1 < len(order):
            weights(k + 1, *order[k + 1])
        if k == 4:
            losses()
    for c in [c for _, c in sent] + par_copies + lse_copies:
        c.wait_send()


def local(blocks, query_rows, key_rows, partner):
    query_rows = pltpu.with_memory_space_constraint(query_rows, pltpu.HBM)
    key_rows = pltpu.with_memory_space_constraint(key_rows, pltpu.HBM)
    partner = pltpu.with_memory_space_constraint(partner, pltpu.HBM)
    R, D = query_rows.shape
    T = 2 * R
    RP = (R + LANES - 1) // LANES * LANES
    f32, bf16 = jnp.float32, jnp.bfloat16
    dma = pltpu.SemaphoreType.DMA
    hbm = pl.BlockSpec(memory_space=pltpu.HBM)
    vmem = pl.BlockSpec(memory_space=pltpu.VMEM)
    loss, grads = pl.pallas_call(
        functools.partial(kernel, blocks),
        out_shape=(
            jax.ShapeDtypeStruct((1, R), f32),
            jax.ShapeDtypeStruct((2, R, D), f32),
        ),
        in_specs=[hbm, hbm, hbm],
        out_specs=[vmem, vmem],
        scratch_shapes=[
            pltpu.VMEM((2, WIN, 4 * R, D), bf16),
            pltpu.VMEM((2, WIN, 2, R, T), f32),
            pltpu.VMEM((2, R, LANES), f32),
            pltpu.VMEM((2, R, LANES), f32),
            pltpu.VMEM((2, R, 4 * R), bf16),
            pltpu.VMEM((T, LANES), f32),
            pltpu.VMEM((LANES, RP), f32),
            pltpu.VMEM((2, R, LANES), f32),
            pltpu.VMEM((R, LANES), f32),
            pltpu.VMEM((2, 1, T), f32),
            pltpu.VMEM((2, WIN, 4, 1, T), f32),
            pltpu.VMEM((1, T), f32),
            pltpu.VMEM((4, 1, T), f32),
            pltpu.VMEM((1, R), jnp.int32),
            dma((3,)),
            dma((4, 2, WIN, 2, CHUNKS)),
            dma((2, WIN, 2, CHUNKS)),
            dma((2, WIN, 2, CHUNKS)),
            dma((2, WIN, 4)),
            dma((2, WIN, 4)),
            dma((3,)),
            dma((4,)),
        ],
        compiler_params=pltpu.CompilerParams(
            collective_id=0, has_side_effects=True, vmem_limit_bytes=46 * 1024 * 1024
        ),
        name="window_loss",
    )(query_rows, key_rows, partner)
    factor = float(D) ** -0.5
    return loss.reshape(R), grads[0] * factor, grads[1] * factor


def solution(mesh):
    return jax.shard_map(
        functools.partial(local, mesh.shape["blk"]),
        mesh=mesh,
        in_specs=(P(("blk", "pb"), None), P(("blk", "pb"), None), P("blk", "pb")),
        out_specs=(P(("blk", "pb")), P(("blk", "pb"), None), P(("blk", "pb"), None)),
        check_vma=False,
    )
```
